32 devices in a mesh: blk: 8 (over y, x, core), line: 4 (over z).
Axes of the slice: x: 2, y: 2, z: 4, core: 2. Of those that a mesh axis runs over, the one named last changes fastest.
Arguments:
- state: bfloat16 [32, 88, 256, 128], P('blk', None, 'line'), may hold values from -6 to 6
- speed_in: float32 [32, 256, 128], P('blk', 'line'), may hold values from -1 to 1
- speed_wall: float32 [32, 256, 128], P('blk', 'line'), may hold values from -1 to 1
- density: float32 [32, 256, 128], P('blk', 'line'), may hold values from 0.3 to 3
- rates: bfloat16 [88, 88], replicated, may hold values from -0.625 to 0.625
- wall_op: bfloat16 [256, 256], replicated, may hold values from -0.375 to 0.375
- block_perm: int32 [32], replicated, may hold values from 0 to 31, each once
- patch_src: int32 [32, 2, 16], P('blk', None, 'line'), may hold values from 0 to 63
- patch_flip: int32 [32, 2, 16], P('blk', None, 'line'), may hold values 0 or 1
- patch_wall: int32 [32, 2, 16], P('blk', None, 'line'), may hold values 0 or 1
Outputs:
- next_state: bfloat16 [32, 88, 256, 128], P('blk', None, 'line')
The draws below stay inside these ranges and needn't reach their ends.
Inputs may be any that keep to these rules, and one draw needn't show every extreme that they name: `block_perm`: each block id 0 to 31 stands in exactly one slot. patch_src // 2 is a block id (not a slot) and patch_src % 2 its face; a patch's rows are the same rows of the source face. `patch_flip`: 1 reverses the order of a patch's rows. `patch_wall`: 1 mirrors the face's own cells in place of a neighbour's.
All inputs are finite; a program needn't handle non-finite values. No bound on the sum of `patch_flip` or of `patch_wall` on one device may be relied on, other than what follows from the above.
Results may differ from the reference program's by a relative error of at most 0.0014.
Values may be sent and summed in bfloat16 or wider, within the bound.
No kernel may reach another device: no remote copies, remote signals or barrier semaphores. Data moves between devices by JAX's collectives and lax.ppermute only.
A program may use at most 192 MiB of HBM per device.

```python
import math
import jax
import jax.numpy as jnp
from jax import lax

C = 88
L = 256
P_SIZE = 128
NB = 32
NP = 16


def touch_ends(drawn, rng, low, high):
    longest = drawn.shape.index(max(drawn.shape))
    spots = []
    for shift in (0, 1):
        where = [jax.random.randint(jax.random.fold_in(rng, axis), (), 0, length) for axis, length in enumerate(drawn.shape)]
        where[longest] = (where[longest] + shift) % drawn.shape[longest]
        spots.append(tuple(where))
    return drawn.at[spots[0]].set(low).at[spots[1]].set(high)


def block_levels(key, extent, split, least, top_value):
    level, own = 1.0, jax.random.fold_in(key, 6)
    for axis_at, blocks in split:
        heights = jnp.exp(jax.random.uniform(jax.random.fold_in(own, axis_at), (blocks,), jnp.float32, least / len(split), top_value / len(split)))
        level = level * jnp.repeat(heights, extent[axis_at] // blocks).reshape([-1 if axis == axis_at else 1 for axis in range(len(extent))])
    return level


def noise(rng, dims, deviation, limit, pieces=(), kind=jnp.bfloat16):
    entries = jax.random.normal(rng, dims, jnp.float32) * deviation
    if len(pieces) > 0:
        entries = block_levels(rng, dims, pieces, -0.22, 0.18) * entries
    return jnp.clip(entries, min=-limit, max=limit).astype(kind)


def setup_inputs(seed: int = 0) -> dict:
    key_list = jax.random.split(jax.random.key(seed), 11)
    return {
        "state": noise(key_list[0], (NB, C, L, P_SIZE), 1.0, 6.0, ((0, 8), (2, 4))),
        "speed_in": jnp.clip(jax.random.uniform(key_list[1], (NB, L, P_SIZE), jnp.float32, -1.0, 1.0) * block_levels(key_list[1], (NB, L, P_SIZE), ((0, 8), (1, 4)), -0.4, 0.0), -1.0, 1.0),
        "speed_wall": jnp.clip(jax.random.uniform(key_list[2], (NB, L, P_SIZE), jnp.float32, -1.0, 1.0) * block_levels(key_list[2], (NB, L, P_SIZE), ((0, 8), (1, 4)), -0.4, 0.0), -1.0, 1.0),
        "density": jnp.clip(jnp.exp(math.log(3.0) - 2.3025851 * jax.random.uniform(key_list[3], (NB, L, P_SIZE), jnp.float32) ** block_levels(key_list[3], (NB, L, P_SIZE), ((0, 8), (1, 4)), -0.2, 0.2)), 0.3, 3.0),
        "rates": noise(key_list[4], (C, C), C ** -0.5, 0.625),
        "wall_op": noise(key_list[5], (L, L), L ** -0.5, 0.375),
        "block_perm": jax.random.permutation(key_list[6], NB).astype(jnp.int32),
        "patch_src": touch_ends(jax.random.randint(key_list[7], (NB, 2, NP), 0, 2 * NB), jax.random.fold_in(key_list[7], 1), 0, (2 * NB) - 1).astype(jnp.int32),
        "patch_flip": touch_ends((jax.random.randint(key_list[8], (NB, 2, NP), 0, 2) < 1).astype(jnp.int32), jax.random.fold_in(key_list[8], 1), 0, 1),
        "patch_wall": touch_ends((jax.random.randint(key_list[9], (NB, 2, NP), 0, 4) < 1).astype(jnp.int32), jax.random.fold_in(key_list[9], 1), 0, 1),
    }


filter_sigma = 0.5
section_step = 0.25
deriv_coef = [5.0 / 6.0, -5.0 / 21.0, 5.0 / 84.0, -5.0 / 504.0, 1.0 / 1260.0]
high_pass = [((-1) ** offset) * math.comb(10, 5 + offset) / 1024.0 for offset in range(-5, 6)]


def edge_cells(field):
    columns = field.shape[-1]
    return jnp.stack([field[..., :5], jnp.flip(field[..., columns - 5:], -1)], 1)


def source_faces(block_perm, patch_src, patch_wall, first_slot):
    nblocks = block_perm.shape[0]
    block_ids = jnp.arange(nblocks, dtype=jnp.int32)
    matches = block_perm[None, :] == block_ids[:, None]
    slot_of = jnp.sum(jnp.where(matches, block_ids[None, :], 0), axis=1).astype(jnp.int32)
    owned = patch_src.shape[0]
    own_face = (first_slot + jnp.arange(owned, dtype=jnp.int32))[:, None, None] * 2 + jnp.arange(2, dtype=jnp.int32)[None, :, None]
    remote = jnp.take(slot_of, patch_src // 2) * 2 + patch_src % 2
    return jnp.where(patch_wall == 1, own_face, remote).astype(jnp.int32)


def select_ghosts(gathered, source, flips, patch_count):
    total = gathered.shape[0]
    chans = gathered.shape[2]
    rows = gathered.shape[3]
    flat = gathered.reshape(total * 2, chans, patch_count, rows // patch_count, 5)
    patch_index = jnp.arange(patch_count, dtype=jnp.int32)[None, None, :]
    picked = flat[source, :, patch_index]
    picked = jnp.where(flips[..., None, None, None] == 1, jnp.flip(picked, -2), picked)
    picked = jnp.transpose(picked, (0, 1, 3, 2, 4, 5))
    return picked.reshape(source.shape[0], 2, chans, rows, 5)


def section_update(state, ghosts, normal, speed_in, speed_wall, density, rates):
    values = state.astype(jnp.float32)
    columns = values.shape[-1]
    extended = jnp.concatenate([jnp.flip(ghosts[:, 0].astype(jnp.float32), -1), values, ghosts[:, 1].astype(jnp.float32)], -1)
    smooth = values
    for offset in range(11):
        smooth = smooth - filter_sigma * high_pass[offset] * extended[..., offset:offset + columns]
    slope = jnp.zeros_like(values)
    for offset in range(1, 6):
        slope = slope + deriv_coef[offset - 1] * (extended[..., 5 + offset:5 + offset + columns] - extended[..., 5 - offset:5 - offset + columns])
    mixed = jnp.einsum('ce,belp->bclp', rates.astype(jnp.float32), values)
    residual = -speed_in[:, None] * slope - speed_wall[:, None] * normal + density[:, None] * mixed
    return (smooth + section_step * residual).astype(jnp.bfloat16)


def reference(state, speed_in, speed_wall, density, rates, wall_op, block_perm, patch_src, patch_flip, patch_wall):
    strips = edge_cells(state)
    source = source_faces(block_perm, patch_src, patch_wall, 0)
    ghosts = select_ghosts(strips, source, patch_flip, patch_src.shape[2])
    operator = wall_op.astype(jnp.float32)

    def one_block(items):
        block_state, block_ghost, block_in, block_wall, block_density = items
        normal = jnp.einsum('lm,cmp->clp', operator, block_state.astype(jnp.float32))
        normal = lax.optimization_barrier(normal.astype(jnp.bfloat16)).astype(jnp.float32)
        return section_update(block_state[None], block_ghost[None], normal[None], block_in[None], block_wall[None], block_density[None], rates)[0]

    return lax.map(one_block, (state, ghosts, speed_in, speed_wall, density))
```

```python
import math

import jax
import jax.numpy as jnp
import numpy as np
from jax import lax
from jax.experimental import pallas as pl
from jax.experimental.pallas import tpu as pltpu
from jax.sharding import PartitionSpec as P


filter_sigma = 0.5
section_step = 0.25
deriv_coef = [5.0 / 6.0, -5.0 / 21.0, 5.0 / 84.0, -5.0 / 504.0, 1.0 / 1260.0]
high_pass = [(-1) ** offset * math.comb(10, 5 + offset) / 1024.0 for offset in range(-5, 6)]
DEPTH = 5
SUB = 8
bf16 = jnp.bfloat16
f32 = jnp.float32


def source_faces(block_perm, patch_src, patch_wall, first_slot):
    nblocks = block_perm.shape[0]
    block_ids = jnp.arange(nblocks, dtype=jnp.int32)
    matches = block_perm[None, :] == block_ids[:, None]
    slot_of = jnp.sum(jnp.where(matches, block_ids[None, :], 0), axis=1)
    owned = patch_src.shape[0]
    own_face = (first_slot + jnp.arange(owned, dtype=jnp.int32))[:, None, None] * 2 + jnp.arange(
        2, dtype=jnp.int32
    )[None, :, None]
    remote = jnp.take(slot_of, patch_src // 2) * 2 + patch_src % 2
    return jnp.where(patch_wall == 1, own_face, remote)


def face_selector(columns):
    pick = np.zeros((2 * SUB, columns), np.float32)
    for d in range(DEPTH):
        pick[d, d] = 1.0
        pick[SUB + d, columns - 1 - d] = 1.0
    return pick


def ghost_placer(columns):
    place = np.zeros((2 * SUB, columns), np.float32)
    for d in range(DEPTH):
        place[d, columns - 1 - d] = 1.0
        place[SUB + d, d] = 1.0
    return place


def flip_pair(size, group):
    same = np.eye(size, dtype=np.float32)
    turned = np.zeros((size, size), np.float32)
    for lane in range(size):
        turned[lane, lane // group * group + group - 1 - lane % group] = 1.0
    return np.stack([same, turned])


def pack_strips(state, patches):
    owned, chans, rows, columns = state.shape
    per = rows // patches
    wide = chans * per

    def kernel(pick_ref, x_ref, *refs):
        o_ref = refs[-1]
        for k in range(patches):
            cells = x_ref[0, :, k * per : (k + 1) * per, :].reshape(wide, columns)
            strip = lax.dot_general(
                pick_ref[...], cells, (((1,), (1,)), ((), ())), preferred_element_type=f32
            ).astype(bf16)
            o_ref[0, 0, k] = strip[:SUB]
            o_ref[0, 1, k] = strip[SUB:]

    return pl.pallas_call(
        kernel,
        grid=(owned,),
        in_specs=[
            pl.BlockSpec((2 * SUB, columns), lambda s: (0, 0)),
            pl.BlockSpec((1, chans, rows, columns), lambda s: (s, 0, 0, 0)),
        ],
        out_specs=pl.BlockSpec((1, 2, patches, SUB, wide), lambda s: (s, 0, 0, 0, 0)),
        out_shape=jax.ShapeDtypeStruct((owned, 2, patches, SUB, wide), bf16),
        cost_estimate=pl.CostEstimate(
            flops=2 * 2 * SUB * state.size, bytes_accessed=3 * state.size, transcendentals=0
        ),
        name="pack_strips",
    )(jnp.asarray(face_selector(columns), bf16), state)


def pick_groups(me, groups, first, count, block):
    n, _, rows, columns = groups.shape

    def kernel(me_ref, *refs):
        for j in range(n - 1):
            refs[n - 1 + j][...] = refs[j][0]

    def chosen(j):
        return lambda i, me: (lax.rem(me[0] + j, n), first // block + i, 0, 0)

    size = (n - 1) * count * rows * columns
    return pl.pallas_call(
        kernel,
        grid_spec=pltpu.PrefetchScalarGridSpec(
            num_scalar_prefetch=1,
            grid=(count // block,),
            in_specs=[pl.BlockSpec((1, block, rows, columns), chosen(j)) for j in range(1, n)],
            out_specs=[pl.BlockSpec((block, rows, columns), lambda i, me: (i, 0, 0))] * (n - 1),
        ),
        out_shape=[jax.ShapeDtypeStruct((count, rows, columns), groups.dtype)] * (n - 1),
        cost_estimate=pl.CostEstimate(flops=0, bytes_accessed=4 * size, transcendentals=0),
        name="pick_groups",
    )(me, *[groups] * (n - 1))


def local_part(state, mixed, speed_in, density, strips, source, flips):
    owned, chans, rows, columns = state.shape
    patches = strips.shape[1]
    per = rows // patches
    wide = chans * per
    step = columns // per

    def kernel(src_ref, flip_ref, turn_ref, place_ref, x_ref, m_ref, in_ref, den_ref, g0_ref, g1_ref, *refs):
        o_ref = refs[-1]
        s, k = pl.program_id(0), pl.program_id(1)

        def turned(ref, face):
            block = ref[0, 0].astype(f32)
            stacked = jnp.concatenate(
                [block[:, i * columns : (i + 1) * columns] for i in range(wide // columns)], 0
            ).astype(bf16)
            turn = turn_ref[flip_ref[(s * 2 + face) * patches + k]]
            return jnp.dot(stacked, turn, preferred_element_type=f32)

        low, high = turned(g0_ref, 0), turned(g1_ref, 1)
        lane = lax.broadcasted_iota(jnp.int32, (step * per, columns), 1)
        speed = jnp.broadcast_to(-section_step * in_ref[...], (step, per, columns)).reshape(-1, columns)
        dens = jnp.broadcast_to(section_step * den_ref[...], (step, per, columns)).reshape(-1, columns)
        for i in range(chans // step):
            both = jnp.concatenate([low[i * SUB : (i + 1) * SUB], high[i * SUB : (i + 1) * SUB]], 0)
            ghost = lax.dot_general(
                both.astype(bf16), place_ref[...], (((0,), (0,)), ((), ())), preferred_element_type=f32
            )
            x = x_ref[0, i * step : (i + 1) * step].reshape(step * per, columns).astype(f32)
            smooth = (1.0 - filter_sigma * high_pass[5]) * x
            slope = jnp.zeros_like(x)
            for j in range(1, DEPTH + 1):
                after = pltpu.roll(jnp.where(lane < j, ghost, x), columns - j, 1)
                before = pltpu.roll(jnp.where(lane >= columns - j, ghost, x), j, 1)
                smooth = smooth - (filter_sigma * high_pass[5 + j]) * (after + before)
                slope = slope + deriv_coef[j - 1] * (after - before)
            mix = m_ref[0, i * step : (i + 1) * step].reshape(step * per, columns)
            base = smooth + speed * slope + dens * mix
            o_ref[0, i * step : (i + 1) * step] = base.reshape(step, per, columns)

    def cells(s, k, *_):
        return (s, 0, k, 0)

    def line(s, k, *_):
        return (s, k, 0)

    def ghosts(face):
        return lambda s, k, src, flip: (src[(s * 2 + face) * patches + k], k, 0, 0)

    return pl.pallas_call(
        kernel,
        grid_spec=pltpu.PrefetchScalarGridSpec(
            num_scalar_prefetch=2,
            grid=(owned, patches),
            in_specs=[
                pl.BlockSpec((2, columns, columns), lambda s, k, *_: (0, 0, 0)),
                pl.BlockSpec((2 * SUB, columns), lambda s, k, *_: (0, 0)),
                pl.BlockSpec((1, chans, per, columns), cells),
                pl.BlockSpec((1, chans, per, columns), cells),
                pl.BlockSpec((1, per, columns), line),
                pl.BlockSpec((1, per, columns), line),
                pl.BlockSpec((1, 1, SUB, wide), ghosts(0)),
                pl.BlockSpec((1, 1, SUB, wide), ghosts(1)),
            ],
            out_specs=pl.BlockSpec((1, chans, per, columns), cells),
        ),
        out_shape=jax.ShapeDtypeStruct(state.shape, f32),
        cost_estimate=pl.CostEstimate(
            flops=60 * state.size, bytes_accessed=10 * state.size, transcendentals=0
        ),
        name="local_part",
    )(
        source.reshape(-1),
        flips.reshape(-1),
        jnp.asarray(flip_pair(columns, per), bf16),
        jnp.asarray(ghost_placer(columns), bf16),
        state,
        mixed,
        speed_in,
        density,
        strips,
        strips,
    )


def wall_product(me, groups, operator, arrived, first, block):
    n, _, rows, columns = groups.shape
    count = arrived[0].shape[0]

    def kernel(me_ref, w_ref, own_ref, *refs):
        ins, outs = refs[: n - 1], refs[-n:]
        lines = []
        for i in range(block):
            lines.append(jnp.concatenate([own_ref[0, i]] + [ref[i] for ref in ins], 0))
        whole = jnp.dot(w_ref[...], jnp.concatenate(lines, 1), preferred_element_type=f32).astype(bf16)
        for j in range(n):
            for i in range(block):
                outs[j][i] = whole[j * rows : (j + 1) * rows, i * columns : (i + 1) * columns]

    piece = pl.BlockSpec((block, rows, columns), lambda i, me: (i, 0, 0))
    size = n * count * rows * columns
    return pl.pallas_call(
        kernel,
        grid_spec=pltpu.PrefetchScalarGridSpec(
            num_scalar_prefetch=1,
            grid=(count // block,),
            in_specs=[
                pl.BlockSpec((n * rows, n * rows), lambda i, me: (0, 0)),
                pl.BlockSpec((1, block, rows, columns), lambda i, me: (me[0], first // block + i, 0, 0)),
            ]
            + [piece] * (n - 1),
            out_specs=[piece] * n,
        ),
        out_shape=[jax.ShapeDtypeStruct((count, rows, columns), bf16)] * n,
        cost_estimate=pl.CostEstimate(
            flops=2 * n * rows * size, bytes_accessed=4 * size, transcendentals=0
        ),
        name="wall_product",
    )(me, operator, groups, *arrived)


def finish(me, base, speed_wall, normals, out, first, block):
    n, _, rows, columns = base.shape
    count = normals[0].shape[0]
    per_slot = n // speed_wall.shape[0]
    fresh = out is None

    def kernel(me_ref, speed_ref, base_ref, *refs):
        o_ref = refs[-1]
        for j in range(n):
            group = lax.rem(me_ref[0] + (n - j), n)
            speed = -section_step * speed_ref[group // per_slot]
            o_ref[group] = (base_ref[group] + speed[None] * refs[j][...].astype(f32)).astype(bf16)

    whole = pl.BlockSpec((n, block, rows, columns), lambda i, me: (0, first // block + i, 0, 0))
    size = n * count * rows * columns
    return pl.pallas_call(
        kernel,
        grid_spec=pltpu.PrefetchScalarGridSpec(
            num_scalar_prefetch=1,
            grid=(count // block,),
            in_specs=[pl.BlockSpec(speed_wall.shape, lambda i, me: (0, 0, 0)), whole]
            + [pl.BlockSpec((block, rows, columns), lambda i, me: (i, 0, 0))] * n
            + [pl.BlockSpec(memory_space=pl.ANY)] * (not fresh),
            out_specs=whole,
        ),
        out_shape=jax.ShapeDtypeStruct(base.shape, bf16),
        input_output_aliases={} if fresh else {3 + n: 0},
        cost_estimate=pl.CostEstimate(flops=2 * size, bytes_accessed=8 * size, transcendentals=0),
        name="finish",
    )(me, speed_wall, base, *normals, *([] if fresh else [out]))


def chunk_blocks(blocks):
    if blocks < 4:
        return [1] * blocks
    middle = (blocks - 2) // 2
    return [1, middle, blocks - 2 - middle, 1]


def sizes(n, owned, chans):
    items = owned * chans // n
    return items, max(size for size in range(1, 12) if items % size == 0 and (size == 8 or items % 8))


def body(n, nblk, state, speed_in, speed_wall, density, rates, wall_op, block_perm, patch_src, patch_flip, patch_wall):
    owned, chans, rows, columns = state.shape
    patches = patch_src.shape[2]
    me = lax.axis_index("line")
    mine = lax.axis_index("blk")
    items, block = sizes(n, owned, chans)
    groups = state.reshape(n, items, rows, columns)
    where = me.astype(jnp.int32).reshape(1)
    shifts = [[(i, (i + j) % n) for i in range(n)] for j in range(n)]

    chunks, first = [], 0
    for size in chunk_blocks(items // block):
        chunks.append((first, size * block))
        first += size * block

    def send(pieces):
        came = []
        for j in range(1, n):
            came.append(lax.ppermute(pieces[j - 1], "line", shifts[j]))
        return came

    arrived = []
    for first, count in chunks:
        picked = pick_groups(where, groups, first, count, block)
        arrived.append(send(picked))

    strips = pack_strips(state, patches)
    gathered = [strips]
    for r in range(1, nblk):
        gathered.append(lax.ppermute(strips, "blk", [(i, i ^ r) for i in range(nblk)]))
    gathered = jnp.concatenate(gathered, 0).reshape((nblk * owned * 2,) + strips.shape[2:])
    source = source_faces(block_perm, patch_src, patch_wall, mine * owned)
    per_device = 2 * owned
    held = ((source // per_device) ^ mine) * per_device + source % per_device

    tiles = wall_op.reshape(n, rows, n, rows)[:, :, ::-1]
    tiles = jnp.concatenate([tiles, tiles], 0)
    tiles = lax.dynamic_slice_in_dim(tiles, me, n, 0)
    tiles = jnp.concatenate([tiles, tiles], 2)
    operator = lax.dynamic_slice_in_dim(tiles, n - 1 - me, n, 2).reshape(n * rows, n * rows)

    mixed = jnp.einsum("ce,belp->bclp", rates, state, preferred_element_type=f32)

    base = local_part(state, mixed, speed_in, density, gathered, held.astype(jnp.int32), patch_flip)
    base = base.reshape(n, items, rows, columns)

    returned = []
    for (first, count), came in zip(chunks, arrived):
        products = wall_product(where, groups, operator, came, first, block)
        returned.append([products[0]] + send(products[1:]))
    out = None
    for (first, count), normals in zip(chunks, returned):
        out = finish(where, base, speed_wall, normals, out, first, block)
    return out.reshape(state.shape)


def solution(mesh):
    n, nblk = mesh.shape["line"], mesh.shape["blk"]

    def section(*args):
        return body(n, nblk, *args)

    return jax.shard_map(
        section,
        mesh=mesh,
        in_specs=(
            P("blk", None, "line", None),
            P("blk", "line", None),
            P("blk", "line", None),
            P("blk", "line", None),
            P(),
            P(),
            P(),
            P("blk", None, "line"),
            P("blk", None, "line"),
            P("blk", None, "line"),
        ),
        out_specs=P("blk", None, "line", None),
        check_vma=False,
    )
```

```python
import math

import jax
import jax.numpy as jnp
import numpy as np
from jax import lax
from jax.experimental import pallas as pl
from jax.experimental.pallas import tpu as pltpu
from jax.sharding import PartitionSpec as P


filter_sigma = 0.5
section_step = 0.25
deriv_coef = [5.0 / 6.0, -5.0 / 21.0, 5.0 / 84.0, -5.0 / 504.0, 1.0 / 1260.0]
high_pass = [(-1) ** offset * math.comb(10, 5 + offset) / 1024.0 for offset in range(-5, 6)]
DEPTH = 5
SUB = 8
GRANT = 16 << 20
FULL_GRANT = 60 << 20
SCALE = 2520
bf16 = jnp.bfloat16
f32 = jnp.float32


def source_faces(block_perm, patch_src, patch_wall, first_slot):
    nblocks = block_perm.shape[0]
    block_ids = jnp.arange(nblocks, dtype=jnp.int32)
    matches = block_perm[None, :] == block_ids[:, None]
    slot_of = jnp.sum(jnp.where(matches, block_ids[None, :], 0), axis=1)
    owned = patch_src.shape[0]
    own_face = (first_slot + jnp.arange(owned, dtype=jnp.int32))[:, None, None] * 2 + jnp.arange(
        2, dtype=jnp.int32
    )[None, :, None]
    remote = jnp.take(slot_of, patch_src // 2) * 2 + patch_src % 2
    return jnp.where(patch_wall == 1, own_face, remote)


def face_selector(columns):
    pick = np.zeros((2 * SUB, columns), np.float32)
    for d in range(DEPTH):
        pick[d, d] = 1.0
        pick[SUB + d, columns - 1 - d] = 1.0
    return pick


def bands(columns):
    weights = np.zeros((3, 2 * DEPTH + 1))
    for j in range(-DEPTH, DEPTH + 1):
        weights[0, DEPTH + j] = filter_sigma * high_pass[DEPTH + j]
        if j:
            whole = round(deriv_coef[abs(j) - 1] * SCALE)
            rest = int(math.fmod(whole, 2048)) if abs(whole) > 2048 else 0
            weights[1, DEPTH + j] = math.copysign(1, j) * (whole - rest)
            weights[2, DEPTH + j] = math.copysign(1, j) * rest
    inner = np.zeros((columns, 3 * columns), np.float32)
    outer = np.zeros((2 * SUB, 3 * columns), np.float32)
    for band in range(3):
        for p in range(columns):
            for j in range(-DEPTH, DEPTH + 1):
                q = p + j
                weight = weights[band, DEPTH + j]
                if q < 0:
                    outer[-1 - q, band * columns + p] = weight
                elif q >= columns:
                    outer[SUB + q - columns, band * columns + p] = weight
                else:
                    inner[q, band * columns + p] = weight
    return inner, outer


def flip_pair(size, group):
    same = np.eye(size, dtype=np.float32)
    turned = np.zeros((size, size), np.float32)
    for lane in range(size):
        turned[lane, lane // group * group + group - 1 - lane % group] = 1.0
    return np.stack([same, turned])


def pack_strips(state, patches):
    owned, chans, rows, columns = state.shape
    per = rows // patches
    wide = chans * per

    def kernel(pick_ref, x_ref, *refs):
        o_ref = refs[-1]
        for k in range(patches):
            cells = x_ref[0, :, k * per : (k + 1) * per, :].reshape(wide, columns)
            strip = lax.dot_general(
                pick_ref[...], cells, (((1,), (1,)), ((), ())), preferred_element_type=f32
            ).astype(bf16)
            o_ref[0, 0, k] = strip[:SUB]
            o_ref[0, 1, k] = strip[SUB:]

    return pl.pallas_call(
        kernel,
        grid=(owned,),
        in_specs=[
            pl.BlockSpec((2 * SUB, columns), lambda s: (0, 0)),
            pl.BlockSpec((1, chans, rows, columns), lambda s: (s, 0, 0, 0)),
        ],
        out_specs=pl.BlockSpec((1, 2, patches, SUB, wide), lambda s: (s, 0, 0, 0, 0)),
        out_shape=jax.ShapeDtypeStruct((owned, 2, patches, SUB, wide), bf16),
        cost_estimate=pl.CostEstimate(
            flops=2 * 2 * SUB * state.size, bytes_accessed=3 * state.size, transcendentals=0
        ),
        compiler_params=pltpu.CompilerParams(vmem_limit_bytes=FULL_GRANT),
        name="pack_strips",
    )(jnp.asarray(face_selector(columns), bf16), state)


def pick_groups(me, groups, first, count):
    n, _, rows, columns = groups.shape

    def kernel(me_ref, groups_ref, *refs):
        copies = []
        for j in range(1, n):
            part = groups_ref.at[me_ref[0] ^ j, pl.ds(first, count)]
            copies.append(pltpu.make_async_copy(part, refs[j - 1], refs[-1].at[j - 1]))
            copies[-1].start()
        for copy in copies:
            copy.wait()

    size = (n - 1) * count * rows * columns
    return pl.pallas_call(
        kernel,
        in_specs=[
            pl.BlockSpec(memory_space=pltpu.SMEM),
            pl.BlockSpec(memory_space=pltpu.HBM),
        ],
        out_specs=[pl.BlockSpec(memory_space=pltpu.VMEM)] * (n - 1),
        out_shape=[jax.ShapeDtypeStruct((count, rows, columns), groups.dtype)] * (n - 1),
        scratch_shapes=[pltpu.SemaphoreType.DMA((n - 1,))],
        cost_estimate=pl.CostEstimate(flops=0, bytes_accessed=4 * size, transcendentals=0),
        compiler_params=pltpu.CompilerParams(vmem_limit_bytes=FULL_GRANT),
        name="pick_groups",
    )(me, groups)


def local_part(state, rates, speed_in, density, strips, source, flips):
    owned, chans, rows, columns = state.shape
    patches = strips.shape[1]
    per = rows // patches
    wide = chans * per
    step = columns // per
    inner, outer = bands(columns)

    def kernel(
        src_ref, flip_ref, turn_ref, inner_ref, outer_ref, rates_ref, x_ref, in_ref, den_ref, g0_ref, g1_ref,
        o_ref, plain, mixed,
    ):
        s, k = pl.program_id(0), pl.program_id(1)

        def turned(ref, face):
            block = ref[0, 0].astype(f32)
            stacked = jnp.concatenate(
                [block[:, i * columns : (i + 1) * columns] for i in range(wide // columns)], 0
            ).astype(bf16)
            turn = turn_ref[flip_ref[(s * 2 + face) * patches + k]]
            return jnp.dot(stacked, turn, preferred_element_type=f32)

        low, high = turned(g0_ref, 0), turned(g1_ref, 1)
        plain[...] = x_ref[0].reshape(wide, columns).astype(f32)
        for r in range(0, per, 2):
            pair = [plain[pl.ds(r + i, chans, stride=per), :] for i in range(2)]
            both = jnp.concatenate(pair, 1).astype(bf16)
            mix = jnp.dot(rates_ref[...], both, preferred_element_type=f32)
            for i in range(2):
                mixed[pl.ds(r + i, chans, stride=per), :] = mix[:, i * columns : (i + 1) * columns]
        scale = -section_step / SCALE
        speed = jnp.broadcast_to(scale * in_ref[...], (step, per, columns)).reshape(-1, columns)
        dens = jnp.broadcast_to(section_step * den_ref[...], (step, per, columns)).reshape(-1, columns)
        for i in range(chans // step):
            ghost = jnp.concatenate([low[i * SUB : (i + 1) * SUB], high[i * SUB : (i + 1) * SUB]], 0)
            cells = x_ref[0, i * step : (i + 1) * step].reshape(step * per, columns)
            swept = jnp.dot(cells, inner_ref[...], preferred_element_type=f32) + lax.dot_general(
                ghost.astype(bf16), outer_ref[...], (((0,), (0,)), ((), ())), preferred_element_type=f32
            )
            high_part = swept[:, :columns]
            slope = swept[:, columns : 2 * columns] + swept[:, 2 * columns :]
            here = pl.ds(i * step * per, step * per)
            base = plain[here, :] - high_part + speed * slope + dens * mixed[here, :]
            o_ref[0, i * step : (i + 1) * step] = base.reshape(step, per, columns)

    def cells(s, k, *_):
        return (s, 0, k, 0)

    def line(s, k, *_):
        return (s, k, 0)

    def fixed(s, k, *_):
        return (0, 0)

    def ghosts(face):
        return lambda s, k, src, flip: (src[(s * 2 + face) * patches + k], k, 0, 0)

    return pl.pallas_call(
        kernel,
        grid_spec=pltpu.PrefetchScalarGridSpec(
            num_scalar_prefetch=2,
            grid=(owned, patches),
            in_specs=[
                pl.BlockSpec((2, columns, columns), lambda s, k, *_: (0, 0, 0)),
                pl.BlockSpec(inner.shape, fixed),
                pl.BlockSpec(outer.shape, fixed),
                pl.BlockSpec(rates.shape, fixed),
                pl.BlockSpec((1, chans, per, columns), cells),
                pl.BlockSpec((1, per, columns), line),
                pl.BlockSpec((1, per, columns), line),
                pl.BlockSpec((1, 1, SUB, wide), ghosts(0)),
                pl.BlockSpec((1, 1, SUB, wide), ghosts(1)),
            ],
            out_specs=pl.BlockSpec((1, chans, per, columns), cells),
            scratch_shapes=[pltpu.VMEM((wide, columns), f32), pltpu.VMEM((wide, columns), f32)],
        ),
        out_shape=jax.ShapeDtypeStruct(state.shape, f32),
        cost_estimate=pl.CostEstimate(
            flops=1000 * state.size, bytes_accessed=8 * state.size, transcendentals=0
        ),
        compiler_params=pltpu.CompilerParams(vmem_limit_bytes=GRANT),
        name="local_part",
    )(
        source.reshape(-1),
        flips.reshape(-1),
        jnp.asarray(flip_pair(columns, per), bf16),
        jnp.asarray(inner, bf16),
        jnp.asarray(outer, bf16),
        rates,
        state,
        speed_in,
        density,
        strips,
        strips,
    )


def wall_product(me, groups, operator, arrived, first, block):
    n, _, rows, columns = groups.shape
    count = arrived[0].shape[0]

    def kernel(me_ref, w_ref, own_ref, *refs):
        ins, outs = refs[: n - 1], refs[-n:]
        lines = []
        for i in range(block):
            lines.append(jnp.concatenate([own_ref[0, i]] + [ref[i] for ref in ins], 0))
        whole = jnp.dot(w_ref[...], jnp.concatenate(lines, 1), preferred_element_type=f32).astype(bf16)
        for j in range(n):
            for i in range(block):
                outs[j][i] = whole[j * rows : (j + 1) * rows, i * columns : (i + 1) * columns]

    piece = pl.BlockSpec((block, rows, columns), lambda i, me: (i, 0, 0))
    size = n * count * rows * columns
    return pl.pallas_call(
        kernel,
        grid_spec=pltpu.PrefetchScalarGridSpec(
            num_scalar_prefetch=1,
            grid=(count // block,),
            in_specs=[
                pl.BlockSpec((n * rows, n * rows), lambda i, me: (0, 0)),
                pl.BlockSpec((1, block, rows, columns), lambda i, me: (me[0], first // block + i, 0, 0)),
            ]
            + [piece] * (n - 1),
            out_specs=[piece] * n,
        ),
        out_shape=[jax.ShapeDtypeStruct((count, rows, columns), bf16)] * n,
        cost_estimate=pl.CostEstimate(
            flops=2 * n * rows * size, bytes_accessed=4 * size, transcendentals=0
        ),
        compiler_params=pltpu.CompilerParams(vmem_limit_bytes=GRANT),
        name="wall_product",
    )(me, operator, groups, *arrived)


def finish(me, base, speed_wall, normals, out, first, block):
    n, _, rows, columns = base.shape
    count = normals[0].shape[0]
    per_slot = n // speed_wall.shape[0]
    fresh = out is None

    def kernel(me_ref, speed_ref, base_ref, *refs):
        o_ref = refs[-1]
        for j in range(n):
            group = me_ref[0] ^ j
            speed = -section_step * speed_ref[group // per_slot]
            o_ref[group] = (base_ref[group] + speed[None] * refs[j][...].astype(f32)).astype(bf16)

    whole = pl.BlockSpec((n, block, rows, columns), lambda i, me: (0, first // block + i, 0, 0))
    size = n * count * rows * columns
    return pl.pallas_call(
        kernel,
        grid_spec=pltpu.PrefetchScalarGridSpec(
            num_scalar_prefetch=1,
            grid=(count // block,),
            in_specs=[pl.BlockSpec(speed_wall.shape, lambda i, me: (0, 0, 0)), whole]
            + [pl.BlockSpec((block, rows, columns), lambda i, me: (i, 0, 0))] * n
            + [pl.BlockSpec(memory_space=pl.ANY)] * (not fresh),
            out_specs=whole,
        ),
        out_shape=jax.ShapeDtypeStruct(base.shape, bf16),
        input_output_aliases={} if fresh else {3 + n: 0},
        cost_estimate=pl.CostEstimate(flops=2 * size, bytes_accessed=8 * size, transcendentals=0),
        compiler_params=pltpu.CompilerParams(vmem_limit_bytes=GRANT),
        name="finish",
    )(me, speed_wall, base, *normals, *([] if fresh else [out]))


def finish_last(me, base, speed_wall, normals, out, first):
    n, count, rows, columns = base.shape
    per_slot = n // speed_wall.shape[0]

    def kernel(me_ref, speed_ref, base_ref, *refs):
        o_ref, done, sems = refs[n + 1], refs[n + 2], refs[n + 3]
        copies = []
        for j in range(n):
            group = me_ref[0] ^ j
            speed = -section_step * speed_ref[group // per_slot]
            done[j] = (base_ref[group] + speed[None] * refs[j][...].astype(f32)).astype(bf16)
            copies.append(
                pltpu.make_async_copy(done.at[j], o_ref.at[group, pl.ds(first, count)], sems.at[j])
            )
            copies[-1].start()
        for copy in copies:
            copy.wait()

    here = pl.BlockSpec(memory_space=pltpu.VMEM)
    size = n * count * rows * columns
    return pl.pallas_call(
        kernel,
        in_specs=[pl.BlockSpec(memory_space=pltpu.SMEM)]
        + [here] * (n + 2)
        + [pl.BlockSpec(memory_space=pl.ANY)],
        out_specs=pl.BlockSpec(memory_space=pl.ANY),
        out_shape=jax.ShapeDtypeStruct(out.shape, bf16),
        scratch_shapes=[pltpu.VMEM((n, count, rows, columns), bf16), pltpu.SemaphoreType.DMA((n,))],
        input_output_aliases={3 + n: 0},
        cost_estimate=pl.CostEstimate(flops=2 * size, bytes_accessed=8 * size, transcendentals=0),
        compiler_params=pltpu.CompilerParams(vmem_limit_bytes=GRANT),
        name="finish_last",
    )(me, speed_wall, base, *normals, out)


def chunk_blocks(blocks):
    if blocks < 5:
        return [1] * blocks
    middle = (blocks - 3) // 2
    return [1, middle, blocks - 3 - middle, 1, 1]


def sizes(n, owned, chans):
    items = owned * chans // n
    return items, max(size for size in range(1, 12) if items % size == 0 and (size == 8 or items % 8))


def body(n, nblk, state, speed_in, speed_wall, density, rates, wall_op, block_perm, patch_src, patch_flip, patch_wall):
    owned, chans, rows, columns = state.shape
    patches = patch_src.shape[2]
    me = lax.axis_index("line")
    mine = lax.axis_index("blk")
    items, block = sizes(n, owned, chans)
    groups = state.reshape(n, items, rows, columns)
    where = me.astype(jnp.int32).reshape(1)
    partners = [[(i, i ^ j) for i in range(n)] for j in range(n)]

    chunks, first = [], 0
    for size in chunk_blocks(items // block):
        chunks.append((first, size * block))
        first += size * block

    def send(pieces):
        came = []
        for j in range(1, n):
            came.append(lax.ppermute(pieces[j - 1], "line", partners[j]))
        return came

    arrived = []
    for first, count in chunks:
        picked = pick_groups(where, groups, first, count)
        arrived.append(send(picked))

    strips = pack_strips(state, patches)
    gathered = [strips]
    for r in range(1, nblk):
        gathered.append(lax.ppermute(strips, "blk", [(i, i ^ r) for i in range(nblk)]))
    gathered = jnp.concatenate(gathered, 0).reshape((nblk * owned * 2,) + strips.shape[2:])
    source = source_faces(block_perm, patch_src, patch_wall, mine * owned)
    per_device = 2 * owned
    held = ((source // per_device) ^ mine) * per_device + source % per_device

    place = jnp.arange(n * rows, dtype=jnp.int32)
    moved = (((place // rows) ^ me) * rows + place % rows)[:, None] == place[None, :]
    moved = moved.astype(bf16)
    operator = jnp.dot(moved, wall_op, preferred_element_type=f32).astype(bf16)
    operator = jnp.dot(operator, moved, preferred_element_type=f32).astype(bf16)

    base = local_part(state, rates, speed_in, density, gathered, held.astype(jnp.int32), patch_flip)
    base = base.reshape(n, items, rows, columns)
    tail = lax.slice_in_dim(base, chunks[-1][0], items, axis=1)

    returned = []
    for (first, count), came in zip(chunks, arrived):
        products = wall_product(where, groups, operator, came, first, block)
        returned.append([products[0]] + send(products[1:]))
    out = None
    for k, ((first, count), normals) in enumerate(zip(chunks, returned)):
        if k < len(chunks) - 1:
            out = finish(where, base, speed_wall, normals, out, first, block)
        else:
            out = finish_last(where, tail, speed_wall, normals, out, first)
    return out.reshape(state.shape)


def solution(mesh):
    n, nblk = mesh.shape["line"], mesh.shape["blk"]

    def section(*args):
        return body(n, nblk, *args)

    return jax.shard_map(
        section,
        mesh=mesh,
        in_specs=(
            P("blk", None, "line", None),
            P("blk", "line", None),
            P("blk", "line", None),
            P("blk", "line", None),
            P(),
            P(),
            P(),
            P("blk", None, "line"),
            P("blk", None, "line"),
            P("blk", None, "line"),
        ),
        out_specs=P("blk", None, "line", None),
        check_vma=False,
    )
```
